512 devices in a mesh: section: 16 (over x, y), tp: 32 (over z, core).
Axes of the slice: x: 4, y: 4, z: 16, core: 2. Of those that a mesh axis runs over, the one named last changes fastest.
Arguments:
- sent_act: bfloat16 [16, 512, 8192], P('section', None, 'tp'), may hold values from -60 to 60
- stash: bfloat16 [16, 512, 8192], P('section', None, 'tp'), may hold values from -60 to 60
- grad_back: bfloat16 [16, 512, 8192], P('section', None, 'tp'), may hold values from -6 to 6
- gain: float32 [16, 8192], P('section', 'tp'), may hold values from 0.25 to 1.75
- self_blocks: bfloat16 [16, 2, 6, 8192, 128], P('section', None, None, 'tp'), may hold values from -0.375 to 0.375
- partner_blocks: bfloat16 [16, 2, 6, 8192, 128], P('section', None, None, 'tp'), may hold values from -0.375 to 0.375
- block_mask: int32 [16, 2, 6, 64], P('section', None, None, 'tp'), may hold values 0 or 1
Outputs:
- out_act: bfloat16 [16, 512, 8192], P('section', None, 'tp')
- grad_in: bfloat16 [16, 512, 8192], P('section', None, 'tp')
- grad_self: bfloat16 [16, 2, 6, 8192, 128], P('section', None, None, 'tp')
- grad_partner: bfloat16 [16, 2, 6, 8192, 128], P('section', None, None, 'tp')
- grad_gain: float32 [16, 8192], P('section', 'tp')
The draws below stay inside these ranges and needn't reach their ends.
All inputs are finite; a program needn't handle non-finite values. No bound on the sum of `block_mask` on one device may be relied on, other than what follows from the above.
Results may differ from the reference program's by a relative error of at most 0.02.
Values may be sent and summed in bfloat16 or wider, within the bound.
A program may use at most 64 MiB of HBM per device.

```python
import jax
import jax.numpy as jnp
from jax import lax

D = 8192
BLOCK = 128
FACTORS = 6
TOK = 512
SECTIONS = 16
BLOCKS = 64


def activation_draw(key, salt):
    key = jax.random.fold_in(key, salt)
    first, second, third = jax.random.split(key, 3)
    columns = jnp.arange(D, dtype=jnp.float32) / D
    column_noise = jnp.exp(jax.random.uniform(second, (D,), jnp.float32, -1.15, 1.15))
    row_scale = jnp.exp(jax.random.uniform(third, (SECTIONS, TOK, 1), jnp.float32, -1.15, 1.15))
    rise = jnp.exp(jnp.log(3.0) * columns) / 3.0
    base = jnp.clip(jax.random.normal(first, (SECTIONS, TOK, D), jnp.float32), -4.0, 4.0)
    return base * row_scale * column_noise[None, None, :] * rise[None, None, :]


def draw_sent_act(key, part):
    return activation_draw(key, 11).astype(jnp.bfloat16)


def draw_stash(key, part):
    return activation_draw(key, 23).astype(jnp.bfloat16)


def with_ends(drawn, stream_key, smallest, top_value):
    extent = drawn.shape
    spot = [jax.random.randint(jax.random.fold_in(stream_key, axis), (), 0, extent[axis]) for axis in range(len(extent))]
    drawn = drawn.at[tuple(spot)].set(smallest)
    longest = extent.index(max(extent))
    spot[longest] = (spot[longest] + 1) % extent[longest]
    return drawn.at[tuple(spot)].set(top_value)


def block_scale(key, extent, cuts, low, top_value):
    loudness, own = 1.0, jax.random.fold_in(key, 6)
    for axis_at, blocks in cuts:
        draws = jnp.exp(jax.random.uniform(jax.random.fold_in(own, axis_at), (blocks,), jnp.float32, low / len(cuts), top_value / len(cuts)))
        loudness = loudness * jnp.repeat(draws, extent[axis_at] // blocks).reshape([-1 if axis == axis_at else 1 for axis in range(len(extent))])
    return loudness


def gaussian(own_key, dims, spread, most, pieces=(), kind=jnp.bfloat16):
    level = block_scale(own_key, dims, pieces, -0.22, 0.18) if pieces else 1.0
    values = jax.random.normal(own_key, dims, jnp.float32) * spread * level
    return jnp.minimum(jnp.maximum(values, -most), most).astype(kind)


def setup_inputs(seed: int = 0) -> dict:
    streams_of = jax.random.split(jax.random.key(seed), 8)
    sent_act = draw_sent_act(jax.random.fold_in(streams_of[7], 71), 0)
    stash = draw_stash(jax.random.fold_in(streams_of[7], 71), 0)
    grad_back = gaussian(streams_of[2], (SECTIONS, TOK, D), 1.0, 6.0, ((0, 16), (2, 32)))
    gain = jnp.clip(1.0 + 0.15 * jax.random.normal(streams_of[3], (SECTIONS, D), jnp.float32), 0.25, 1.75)
    self_blocks = gaussian(streams_of[4], (SECTIONS, 2, FACTORS, D, BLOCK), (2 * BLOCK) ** -0.5, 0.375, ((0, 16), (3, 32)))
    partner_blocks = gaussian(streams_of[5], (SECTIONS, 2, FACTORS, D, BLOCK), (2 * BLOCK) ** -0.5, 0.375, ((0, 16), (3, 32)))
    block_mask = with_ends((jax.random.randint(streams_of[6], (SECTIONS, 2, FACTORS, BLOCKS), 0, 4) < 3).astype(jnp.int32), jax.random.fold_in(streams_of[6], 1), 0, 1)
    return {"sent_act": sent_act, "stash": stash, "grad_back": grad_back, "gain": gain, "self_blocks": self_blocks, "partner_blocks": partner_blocks, "block_mask": block_mask}


EPSILON = 1e-05
GELU_C = 0.7978845608028654
GELU_A = 0.044715

def gelu_value(v):
    inner = GELU_C * (v + GELU_A * v * v * v)
    return 0.5 * v * (1.0 + jnp.tanh(inner))

def gelu_slope(v):
    inner = GELU_C * (v + GELU_A * v * v * v)
    tanh_val = jnp.tanh(inner)
    return 0.5 * (1.0 + tanh_val) + 0.5 * v * (1.0 - tanh_val * tanh_val) * GELU_C * (1.0 + 3.0 * GELU_A * v * v)

def flip_blocks(x, k, axis):
    shape = x.shape
    low = 2 ** k
    parts = shape[:axis] + (shape[axis] // (2 * low), 2, low) + shape[axis + 1:]
    return jnp.flip(x.reshape(parts), axis + 1).reshape(shape)

def normalize(x, gain_row):
    values = x.astype(jnp.float32)
    squares = lax.optimization_barrier(jnp.sum(values * values, axis=1))
    scale = lax.rsqrt(squares / D + EPSILON)
    scaled = values * scale[:, None]
    return ((scaled * gain_row[None, :]).astype(jnp.bfloat16), scaled, scale)

def butterfly(v, selfw, partw, mask):
    inputs = []
    partners = []
    for k in range(FACTORS):
        other = flip_blocks(v, k, 1)
        inputs.append(v)
        partners.append(other)
        own = jnp.einsum('tlc,lcd->tld', v.astype(jnp.float32), selfw[k])
        cross = jnp.einsum('tlc,lcd->tld', other.astype(jnp.float32), partw[k])
        v = (own + mask[k][None, :, None] * cross).astype(jnp.bfloat16)
    return (v, inputs, partners)

def butterfly_back(g, inputs, partners, selfw, partw, mask):
    grads_self = []
    grads_part = []
    for k in reversed(range(FACTORS)):
        grad_f = g.astype(jnp.float32)
        grads_self.append(jnp.einsum('tlc,tld->lcd', inputs[k].astype(jnp.float32), grad_f))
        grads_part.append(mask[k][:, None, None] * jnp.einsum('tlc,tld->lcd', partners[k].astype(jnp.float32), grad_f))
        own = jnp.einsum('tld,lcd->tlc', grad_f, selfw[k])
        term = mask[k][None, :, None] * jnp.einsum('tld,lcd->tlc', grad_f, partw[k])
        g = (own + flip_blocks(term, k, 1)).astype(jnp.bfloat16)
    grads_self = grads_self[::-1]
    grads_part = grads_part[::-1]
    return (g, jnp.stack(grads_self), jnp.stack(grads_part))

def section_step(items):
    x, xs, grad_y, gain_row, self_raw, part_raw, mask_raw = items
    selfw = self_raw.astype(jnp.float32).reshape(2, FACTORS, BLOCKS, BLOCK, BLOCK)
    partw = part_raw.astype(jnp.float32).reshape(2, FACTORS, BLOCKS, BLOCK, BLOCK)
    mask = mask_raw.astype(jnp.float32)
    u, unused_a, unused_b = normalize(x, gain_row)
    a, unused_c, unused_d = butterfly(u.reshape(TOK, BLOCKS, BLOCK), selfw[0], partw[0], mask[0])
    h = gelu_value(a.astype(jnp.float32)).astype(jnp.bfloat16)
    c, unused_e, unused_f = butterfly(h, selfw[1], partw[1], mask[1])
    out = (x.astype(jnp.float32) + c.reshape(TOK, D).astype(jnp.float32)).astype(jnp.bfloat16)
    u_s, scaled_s, scale_s = normalize(xs, gain_row)
    a_s, in_first, par_first = butterfly(u_s.reshape(TOK, BLOCKS, BLOCK), selfw[0], partw[0], mask[0])
    h_s = gelu_value(a_s.astype(jnp.float32)).astype(jnp.bfloat16)
    unused_g, in_second, par_second = butterfly(h_s, selfw[1], partw[1], mask[1])
    dh, gs_second, gp_second = butterfly_back(grad_y.reshape(TOK, BLOCKS, BLOCK), in_second, par_second, selfw[1], partw[1], mask[1])
    da = (dh.astype(jnp.float32) * gelu_slope(a_s.astype(jnp.float32))).astype(jnp.bfloat16)
    du, gs_first, gp_first = butterfly_back(da, in_first, par_first, selfw[0], partw[0], mask[0])
    du_flat = du.reshape(TOK, D).astype(jnp.float32)
    grad_gain = lax.optimization_barrier(jnp.sum(du_flat * scaled_s, axis=0))
    q_val = du_flat * gain_row[None, :]
    corr = lax.optimization_barrier(jnp.sum(q_val * scaled_s, axis=1))
    grad_in = (grad_y.astype(jnp.float32) + scale_s[:, None] * (q_val - scaled_s * corr[:, None] / D)).astype(jnp.bfloat16)
    grad_self = jnp.stack([gs_first, gs_second]).reshape(2, FACTORS, D, BLOCK).astype(jnp.bfloat16)
    grad_partner = jnp.stack([gp_first, gp_second]).reshape(2, FACTORS, D, BLOCK).astype(jnp.bfloat16)
    return (out, grad_in, grad_self, grad_partner, grad_gain)

def reference(sent_act, stash, grad_back, gain, self_blocks, partner_blocks, block_mask):
    arriving = jnp.roll(sent_act, 1, axis=0)
    returning = jnp.roll(grad_back, -1, axis=0)
    out_act, grad_in, grad_self, grad_partner, grad_gain = lax.map(section_step, (arriving, stash, returning, gain, self_blocks, partner_blocks, block_mask))
    return (out_act, grad_in, grad_self, grad_partner, grad_gain)
```

```python
import jax
import jax.numpy as jnp
from jax import lax
from jax.sharding import PartitionSpec as P

D = 8192


EPSILON = 1e-05
GELU_C = 0.7978845608028654
GELU_A = 0.044715


def from_partner(value, axis, apart):
    mask = 2**apart
    pairs = [(source, source ^ mask) for source in range(lax.axis_size(axis))]
    return lax.ppermute(value, axis, pairs)


def from_behind(value, axis, steps):
    count = lax.axis_size(axis)
    pairs = [(source, (source + steps) % count) for source in range(count)]
    return lax.ppermute(value, axis, pairs)


def gelu_value(v):
    inner = GELU_C * (v + GELU_A * v * v * v)
    return 0.5 * v * (1.0 + jnp.tanh(inner))


def gelu_slope(v):
    inner = GELU_C * (v + GELU_A * v * v * v)
    tanh_val = jnp.tanh(inner)
    return 0.5 * (1.0 + tanh_val) + 0.5 * v * (1.0 - tanh_val * tanh_val) * GELU_C * (
        1.0 + 3.0 * GELU_A * v * v
    )


def flip_blocks(x, k, axis):
    shape = x.shape
    low = 2**k
    parts = shape[:axis] + (shape[axis] // (2 * low), 2, low) + shape[axis + 1 :]
    return jnp.flip(x.reshape(parts), axis + 1).reshape(shape)


def block_mix(values, weights):
    return jnp.einsum("tlc,lcd->tld", values, weights, preferred_element_type=jnp.float32)


def block_back(grads, weights):
    return jnp.einsum("tld,lcd->tlc", grads, weights, preferred_element_type=jnp.float32)


def block_grad(values, grads):
    return jnp.einsum("tlc,tld->lcd", values, grads, preferred_element_type=jnp.float32)


def sum_squares(x):
    values = x.astype(jnp.float32)
    return lax.psum(jnp.sum(values * values, axis=1), "tp")


def factor_forward(values, selfw, partw, mask, k, local_bits, finish):
    if k < local_bits:
        other = flip_blocks(values, k, 1)
    else:
        other = from_partner(values, "tp", k - local_bits)
    if not finish:
        return None, other
    mixed = block_mix(values, selfw[k]) + mask[k][None, :, None] * block_mix(other, partw[k])
    return mixed.astype(jnp.bfloat16), other


def factor_backward(grads, selfw, partw, mask, k, local_bits):
    term = (mask[k][None, :, None] * block_back(grads, partw[k])).astype(jnp.bfloat16)
    if k < local_bits:
        back = flip_blocks(term, k, 1)
    else:
        back = from_partner(term, "tp", k - local_bits)
    own = block_back(grads, selfw[k])
    return (own + back.astype(jnp.float32)).astype(jnp.bfloat16)


def weight_grads(inputs, partners, cots, mask):
    grads_self = jnp.stack([block_grad(v, g).astype(jnp.bfloat16) for v, g in zip(inputs, cots)])
    grads_part = jnp.stack(
        [
            (mask[k][:, None, None] * block_grad(v, g)).astype(jnp.bfloat16)
            for k, (v, g) in enumerate(zip(partners, cots))
        ]
    )
    return grads_self, grads_part


def per_device(sent_act, stash, grad_back, gain, self_blocks, partner_blocks, block_mask):
    tokens = sent_act.shape[1]
    width = sent_act.shape[2]
    block = self_blocks.shape[4]
    factors = self_blocks.shape[2]
    local_blocks = width // block
    local_bits = local_blocks.bit_length() - 1
    selfw = self_blocks[0].reshape(2, factors, local_blocks, block, block)
    partw = partner_blocks[0].reshape(2, factors, local_blocks, block, block)
    mask = block_mask[0].astype(jnp.float32)
    gain_row = gain[0]
    wide = (tokens, local_blocks, block)
    returning = from_behind(grad_back, "section", -1)[0]
    arriving = from_behind(sent_act, "section", 1)[0]
    held = stash[0]
    scale_s = lax.rsqrt(sum_squares(held) / D + EPSILON)[:, None, None]
    scale_a = lax.rsqrt(sum_squares(arriving) / D + EPSILON)[:, None, None]
    s = (held.astype(jnp.float32) * gain_row[None, :]).astype(jnp.bfloat16).reshape(wide)
    a = (arriving.astype(jnp.float32) * gain_row[None, :]).astype(jnp.bfloat16).reshape(wide)
    b = returning.reshape(wide)
    s_in, s_par, b_cot = [[], []], [[], []], [[None] * factors, [None] * factors]
    for p in range(2):
        for k in range(factors):
            r = factors - 1 - k
            b_cot[1 - p][r] = b
            s_in[p].append(s)
            b_next = factor_backward(b, selfw[1 - p], partw[1 - p], mask[1 - p], r, local_bits)
            s_next, other = factor_forward(
                s, selfw[p], partw[p], mask[p], k, local_bits, p == 0 or k + 1 < factors
            )
            s_par[p].append(other)
            a, _ = factor_forward(a, selfw[p], partw[p], mask[p], k, local_bits, True)
            s, b = s_next, b_next
        if p == 0:
            pre_s = s.astype(jnp.float32) * scale_s
            s = gelu_value(pre_s).astype(jnp.bfloat16)
            a = gelu_value(a.astype(jnp.float32) * scale_a).astype(jnp.bfloat16)
            da = b.astype(jnp.float32) * gelu_slope(pre_s)
            corr = lax.psum(jnp.sum(da * pre_s, axis=(1, 2)), "tp")
            b = (da * scale_s).astype(jnp.bfloat16)
    out_act = (arriving.astype(jnp.float32) + a.reshape(tokens, width).astype(jnp.float32)).astype(
        jnp.bfloat16
    )
    gs_first, gp_first = weight_grads(s_in[0], s_par[0], b_cot[0], mask[0])
    gs_second, gp_second = weight_grads(s_in[1], s_par[1], b_cot[1], mask[1])
    du = b.reshape(tokens, width).astype(jnp.float32)
    xs = held.astype(jnp.float32)
    grad_gain = jnp.sum(du * xs, axis=0)
    back = (scale_s[:, 0, 0] * scale_s[:, 0, 0] * corr / D)[:, None]
    grad_in = (returning.astype(jnp.float32) + (du * gain_row[None, :] - xs * back)).astype(
        jnp.bfloat16
    )
    grad_self = jnp.stack([gs_first, gs_second]).reshape(1, 2, factors, width, block)
    grad_partner = jnp.stack([gp_first, gp_second]).reshape(1, 2, factors, width, block)
    return (out_act[None], grad_in[None], grad_self, grad_partner, grad_gain[None])


def solution(mesh):
    in_specs = (
        P("section", None, "tp"),
        P("section", None, "tp"),
        P("section", None, "tp"),
        P("section", "tp"),
        P("section", None, None, "tp", None),
        P("section", None, None, "tp", None),
        P("section", None, None, "tp"),
    )
    out_specs = (
        P("section", None, "tp"),
        P("section", None, "tp"),
        P("section", None, None, "tp", None),
        P("section", None, None, "tp", None),
        P("section", "tp"),
    )
    return jax.shard_map(
        per_device, mesh=mesh, in_specs=in_specs, out_specs=out_specs, check_vma=False
    )
```

```python
import functools

import jax
import jax.numpy as jnp
from jax import lax
from jax.experimental import pallas as pl
from jax.experimental.pallas import tpu as pltpu
from jax.sharding import PartitionSpec as P

EPSILON = 1e-05
GELU_C = 0.7978845608028654
GELU_A = 0.044715
BLOCK = 128
ROWS = 256
MESH = pl.DeviceIdType.MESH
F32 = jnp.float32
BF16 = jnp.bfloat16


def gelu_value(v):
    inner = GELU_C * (v + GELU_A * v * v * v)
    return 0.5 * v * (1.0 + jnp.tanh(inner))


def gelu_slope(v):
    inner = GELU_C * (v + GELU_A * v * v * v)
    tanh_val = jnp.tanh(inner)
    return 0.5 * (1.0 + tanh_val) + 0.5 * v * (1.0 - tanh_val * tanh_val) * GELU_C * (
        1.0 + 3.0 * GELU_A * v * v
    )


def contract(a, b, da, db):
    return lax.dot_general(a, b, (((da,), (db,)), ((), ())), preferred_element_type=F32)


def columns(l):
    return slice(l * BLOCK, (l + 1) * BLOCK)


def kernel(
    sections,
    bits,
    order,
    sent,
    stash,
    gback,
    gain,
    selfw,
    partw,
    out_act,
    grad_in,
    gself,
    gpart,
    ggain,
    arr,
    ret,
    s_v,
    s_o,
    a_v,
    a_o,
    b_g,
    b_t,
    b_o,
    own,
    pre,
    acc,
    rs_col,
    rs_row,
    st_v,
    st_o,
    send_sem,
    recv_sem,
):
    tokens, width = stash.shape
    factors = bits + 1
    last = factors - 1
    rows_step = min(ROWS, tokens)
    total_width = float((2**bits) * width)
    sec = lax.axis_index("section")
    tp = lax.axis_index("tp")
    ahead = lax.rem(sec + 1, sections)
    behind = lax.rem(sec + sections - 1, sections)
    peers = []
    for j in range(bits):
        m = 2**j
        peers.append(tp + m - 2 * m * ((tp // m) % 2))

    barrier = pltpu.get_barrier_semaphore()
    for peer in peers:
        pl.semaphore_signal(barrier, inc=1, device_id=(sec, peer), device_id_type=MESH)
    for other in (ahead, behind):
        pl.semaphore_signal(barrier, inc=1, device_id=(other, tp), device_id_type=MESH)
    pl.semaphore_wait(barrier, bits + 2)

    pending = []

    def send(src, dst, where):
        n = len(pending)
        copy = pltpu.make_async_remote_copy(
            src_ref=src,
            dst_ref=dst,
            send_sem=send_sem.at[n],
            recv_sem=recv_sem.at[n],
            device_id=where,
            device_id_type=MESH,
        )
        copy.start()
        pending.append(copy)
        return copy

    def over_rows(body):
        def one(i, carry):
            body(pl.ds(pl.multiple_of(i * rows_step, rows_step), rows_step))
            return carry

        lax.fori_loop(0, tokens // rows_step, one, 0)

    def local_weights(p):
        f = p * factors
        top = jnp.concatenate([selfw[f, columns(0), :], partw[f, columns(1), :]], axis=1)
        low = jnp.concatenate([partw[f, columns(0), :], selfw[f, columns(1), :]], axis=1)
        return jnp.concatenate([top, low], axis=0)

    def stacked(p, k, l):
        f = p * factors + k
        return jnp.concatenate([selfw[f, columns(l), :], partw[f, columns(l), :]], axis=0)

    def forward(p, k, v, o, emit):
        def body(rows):
            if k == 0:
                both = contract(v[rows, :], local_weights(p), 1, 0)
                for l in range(2):
                    emit(rows, l, both[:, columns(l)])
                return
            for l in range(2):
                lhs = jnp.concatenate([v[rows, columns(l)], o[rows, columns(l)]], axis=1)
                emit(rows, l, contract(lhs, stacked(p, k, l), 1, 0))

        over_rows(body)

    def row_sums(values):
        return jnp.sum(values.T, axis=0, keepdims=True)

    def as_column(row):
        return jnp.broadcast_to(row, (BLOCK, tokens)).T

    class Total:
        def __init__(self, slot):
            self.slot, self.at = slot, 0

        def begin(self, values):
            st_v[self.slot, 0] = row_sums(values)

        def send(self, peer):
            n = self.at
            self.copy = send(st_v.at[self.slot, n], st_o.at[self.slot, n], (sec, peer))

        def absorb(self):
            n = self.at
            self.copy.wait_recv()
            st_v[self.slot, n + 1] = st_v[self.slot, n] + st_o[self.slot, n]
            self.at = n + 1

        def value(self):
            return st_v[self.slot, self.at]

    def scale_of(total):
        return lax.rsqrt(total.value() / total_width + EPSILON)

    def start_norm(x, v, total):
        def body(rows):
            squares = None
            for l in range(2):
                part = x[rows, columns(l)].astype(F32)
                v[rows, columns(l)] = (part * gain[:, columns(l)]).astype(BF16)
                squares = part * part if squares is None else squares + part * part
            acc[rows, :] = squares

        over_rows(body)
        total.begin(acc[...])

    def forward_chain(x, wait_x, v, o, slot, finish_first, finish_second, keep):
        def store(p, k):
            def emit(rows, l, value):
                v[p, k, rows, columns(l)] = value.astype(BF16)

            return emit

        total = Total(slot)
        if wait_x is not None:
            wait_x.wait_recv()
        start_norm(x, v.at[0, 0], total)
        for p in range(2):
            forward(p, 0, v.at[p, 0], None, store(p, 1))
            for k in range(1, factors):
                copy = send(v.at[p, k], o.at[p, k - 1], (sec, peers[k - 1]))
                if p == 0:
                    total.send(peers[k - 1])
                yield
                copy.wait_recv()
                if p == 0:
                    total.absorb()
                if k < last:
                    forward(p, k, v.at[p, k], o.at[p, k - 1], store(p, k + 1))
                elif p == 0:
                    forward(p, k, v.at[p, k], o.at[p, k - 1], finish_first(total))
                elif keep:
                    forward(p, k, v.at[p, k], o.at[p, k - 1], finish_second)
        yield

    def stash_first(total):
        scale = scale_of(total)
        rs_row[...] = scale
        rs_col[...] = as_column(scale)

        def emit(rows, l, value):
            value = value * rs_col[rows, :]
            pre[rows, columns(l)] = value
            s_v[1, 0, rows, columns(l)] = gelu_value(value).astype(BF16)

        return emit

    def arriving_first(total):
        acc[...] = as_column(scale_of(total))

        def emit(rows, l, value):
            a_v[1, 0, rows, columns(l)] = gelu_value(value * acc[rows, :]).astype(BF16)

        return emit

    def arriving_second(rows, l, value):
        out_act[rows, columns(l)] = (arr[rows, columns(l)].astype(F32) + value).astype(BF16)

    def backward_chain():
        from_ahead.wait_recv()
        total = Total(2)
        for p in (1, 0):
            for k in range(last, 0, -1):
                g = ret if (p == 1 and k == last) else b_g.at[p, k]
                term = b_t.at[p, k - 1]

                def split(rows, g=g, term=term, p=p, k=k):
                    for l in range(2):
                        both = contract(g[rows, columns(l)], stacked(p, k, l), 1, 1)
                        own[rows, columns(l)] = both[:, columns(0)]
                        term[rows, columns(l)] = both[:, columns(1)].astype(BF16)

                over_rows(split)
                copy = send(term, b_o.at[p, k - 1], (sec, peers[k - 1]))
                if p == 0:
                    total.send(peers[k - 1])
                yield
                copy.wait_recv()
                if p == 0:
                    total.absorb()

                def join(rows, p=p, k=k):
                    b_g[p, k - 1, rows, :] = (
                        own[rows, :] + b_o[p, k - 1, rows, :].astype(F32)
                    ).astype(BF16)

                over_rows(join)

            if p == 1:

                def middle(rows):
                    dh = contract(b_g[1, 0, rows, :], local_weights(1), 1, 1)
                    products = None
                    for l in range(2):
                        a = pre[rows, columns(l)]
                        da = dh[:, columns(l)] * gelu_slope(a)
                        products = da * a if products is None else products + da * a
                        b_g[0, last, rows, columns(l)] = (da * rs_col[rows, :]).astype(BF16)
                    acc[rows, :] = products

                over_rows(middle)
                total.begin(acc[...])
        scale = rs_row[...]
        acc[...] = as_column(scale * scale * total.value() / total_width)
        ggain[...] = jnp.zeros_like(ggain)

        def finish(rows):
            du = contract(b_g[0, 0, rows, :], local_weights(0), 1, 1)
            for l in range(2):
                part, x = du[:, columns(l)], stash[rows, columns(l)].astype(F32)
                ggain[:, columns(l)] += jnp.sum(part * x, axis=0, keepdims=True)
                value = part * gain[:, columns(l)] - x * acc[rows, :]
                grad_in[rows, columns(l)] = (ret[rows, columns(l)].astype(F32) + value).astype(BF16)

        over_rows(finish)
        yield

    def weight_grads(p, k):
        g = ret if (p == 1 and k == last) else b_g.at[p, k]
        f = p * factors + k
        for l in range(2):
            if k == 0:
                lhs = s_v[p, 0]
            else:
                lhs = jnp.concatenate([s_v[p, k, :, columns(l)], s_o[p, k - 1, :, columns(l)]], axis=1)
            both = contract(lhs, g[:, columns(l)], 0, 0).astype(BF16)
            mine, theirs = (1, 0) if (k == 0 and l == 1) else (0, 1)
            gself[f, columns(l), :] = both[columns(mine), :]
            gpart[f, columns(l), :] = both[columns(theirs), :]

    from_ahead = send(gback, ret, (behind, tp))
    from_behind = send(sent, arr, (ahead, tp))
    chains = {
        "S": forward_chain(stash, None, s_v, s_o, 0, stash_first, None, False),
        "A": forward_chain(arr, from_behind, a_v, a_o, 1, arriving_first, arriving_second, True),
        "B": backward_chain(),
    }
    for name, index in order:
        if name == "G":
            weight_grads(*index)
        else:
            next(chains[name])
    for copy in pending:
        copy.wait_send()


def make_order(bits, lag):
    steps = 2 * bits + 1
    order = []
    for t in range(steps + lag):
        if t < steps:
            order += [("S", t), ("B", t)]
        if t >= lag:
            order.append(("A", t - lag))
        if bits <= t < steps:
            order += [("G", (1, t - bits)), ("G", (0, 2 * bits - t))]
    return order


def solution(mesh):
    sections, shards = mesh.shape["section"], mesh.shape["tp"]
    bits = shards.bit_length() - 1

    def per_device(sent_act, stash, grad_back, gain, self_blocks, partner_blocks, block_mask):
        tokens, width = stash.shape[1:]
        factors = self_blocks.shape[2]
        assert width == 2 * BLOCK and factors == bits + 1
        count = 2 * factors
        mask = block_mask[0].reshape(count, 2, 1, 1).astype(BF16)
        partw = (partner_blocks[0].reshape(count, 2, BLOCK, BLOCK) * mask).reshape(count, width, BLOCK)
        copies = 2 + 6 * bits + 3 * bits
        vmem = pl.BlockSpec(memory_space=pltpu.VMEM)
        out_act, grad_in, gself, gpart, ggain = pl.pallas_call(
            functools.partial(kernel, sections, bits, make_order(bits, 2)),
            out_shape=(
                jax.ShapeDtypeStruct((tokens, width), BF16),
                jax.ShapeDtypeStruct((tokens, width), BF16),
                jax.ShapeDtypeStruct((count, width, BLOCK), BF16),
                jax.ShapeDtypeStruct((count, width, BLOCK), BF16),
                jax.ShapeDtypeStruct((1, width), F32),
            ),
            in_specs=[vmem] * 6,
            out_specs=[vmem] * 5,
            scratch_shapes=[
                pltpu.VMEM((tokens, width), BF16),
                pltpu.VMEM((tokens, width), BF16),
                pltpu.VMEM((2, factors, tokens, width), BF16),
                pltpu.VMEM((2, bits, tokens, width), BF16),
                pltpu.VMEM((2, factors, tokens, width), BF16),
                pltpu.VMEM((2, bits, tokens, width), BF16),
                pltpu.VMEM((2, factors, tokens, width), BF16),
                pltpu.VMEM((2, bits, tokens, width), BF16),
                pltpu.VMEM((2, bits, tokens, width), BF16),
                pltpu.VMEM((tokens, width), F32),
                pltpu.VMEM((tokens, width), F32),
                pltpu.VMEM((tokens, BLOCK), F32),
                pltpu.VMEM((tokens, BLOCK), F32),
                pltpu.VMEM((1, tokens), F32),
                pltpu.VMEM((3, bits + 1, 1, tokens), F32),
                pltpu.VMEM((3, bits, 1, tokens), F32),
                pltpu.SemaphoreType.DMA((copies,)),
                pltpu.SemaphoreType.DMA((copies,)),
            ],
            compiler_params=pltpu.CompilerParams(
                collective_id=0, has_side_effects=True, vmem_limit_bytes=48 * 2**20
            ),
        )(
            sent_act[0],
            stash[0],
            grad_back[0],
            gain,
            self_blocks[0].reshape(count, width, BLOCK),
            partw,
        )
        gpart = (gpart.reshape(count, 2, BLOCK, BLOCK) * mask).reshape(partner_blocks.shape)
        return out_act[None], grad_in[None], gself.reshape(self_blocks.shape), gpart, ggain

    in_specs = (
        P("section", None, "tp"),
        P("section", None, "tp"),
        P("section", None, "tp"),
        P("section", "tp"),
        P("section", None, None, "tp", None),
        P("section", None, None, "tp", None),
        P("section", None, None, "tp"),
    )
    out_specs = (
        P("section", None, "tp"),
        P("section", None, "tp"),
        P("section", None, None, "tp", None),
        P("section", None, None, "tp", None),
        P("section", "tp"),
    )
    return jax.shard_map(per_device, mesh=mesh, in_specs=in_specs, out_specs=out_specs, check_vma=False)
```

```python
import functools

import jax
import jax.numpy as jnp
from jax import lax
from jax.experimental import pallas as pl
from jax.experimental.pallas import tpu as pltpu
from jax.sharding import PartitionSpec as P

EPSILON = 1e-05
GELU_C = 0.7978845608028654
GELU_A = 0.044715
BLOCK = 128
PARTS = 2
ORDER = ""
MESH = pl.DeviceIdType.MESH
F32 = jnp.float32
BF16 = jnp.bfloat16


def gelu_value(v):
    inner = GELU_C * (v + GELU_A * v * v * v)
    return 0.5 * v * (1.0 + jnp.tanh(inner))


def gelu_slope(v):
    inner = GELU_C * (v + GELU_A * v * v * v)
    tanh_val = jnp.tanh(inner)
    return 0.5 * (1.0 + tanh_val) + 0.5 * v * (1.0 - tanh_val * tanh_val) * GELU_C * (
        1.0 + 3.0 * GELU_A * v * v
    )


def contract(a, b, da, db):
    return lax.dot_general(a, b, (((da,), (db,)), ((), ())), preferred_element_type=F32)


def columns(l):
    return slice(l * BLOCK, (l + 1) * BLOCK)


def kernel(
    sections,
    bits,
    order,
    sent,
    stash,
    gback,
    gain,
    selfw,
    partw,
    out_act,
    grad_in,
    gself,
    gpart,
    ggain,
    arr,
    ret,
    s_v,
    s_o,
    a_v,
    a_o,
    b_g,
    b_t,
    b_o,
    own,
    pre,
    acc,
    rs_col,
    rs_row,
    st_v,
    st_o,
    far_w,
    far_out,
    far_in,
    send_sem,
    recv_sem,
):
    tokens, width = stash.shape
    part_rows = tokens // PARTS
    factors = bits + 1
    last = factors - 1
    total_width = float((2**bits) * width)
    sec = lax.axis_index("section")
    tp = lax.axis_index("tp")
    ahead = lax.rem(sec + 1, sections)
    behind = lax.rem(sec + sections - 1, sections)
    peers = []
    for j in range(bits):
        m = 2**j
        peers.append(tp + m - 2 * m * ((tp // m) % 2))

    barrier = pltpu.get_barrier_semaphore()
    for peer in peers:
        pl.semaphore_signal(barrier, inc=1, device_id=(sec, peer), device_id_type=MESH)
    for other in (ahead, behind):
        pl.semaphore_signal(barrier, inc=1, device_id=(other, tp), device_id_type=MESH)
    pl.semaphore_wait(barrier, bits + 2)

    pending = []

    def send(src, dst, where):
        n = len(pending)
        copy = pltpu.make_async_remote_copy(
            src_ref=src,
            dst_ref=dst,
            send_sem=send_sem.at[n],
            recv_sem=recv_sem.at[n],
            device_id=where,
            device_id_type=MESH,
        )
        copy.start()
        pending.append(copy)
        return copy

    def rows_of(h):
        return slice(h * part_rows, (h + 1) * part_rows)

    def local_weights(p):
        f = p * factors
        top = jnp.concatenate([selfw[f, columns(0), :], partw[f, columns(1), :]], axis=1)
        low = jnp.concatenate([partw[f, columns(0), :], selfw[f, columns(1), :]], axis=1)
        return jnp.concatenate([top, low], axis=0)

    def stacked(p, k, l):
        f = p * factors + k
        return jnp.concatenate([selfw[f, columns(l), :], partw[f, columns(l), :]], axis=0)

    def row_sums(values):
        return jnp.sum(values.T, axis=0, keepdims=True)

    def as_column(row):
        return jnp.broadcast_to(row, (BLOCK, part_rows)).T

    class Total:
        def __init__(self, slot):
            self.slot, self.at = slot, 0

        def begin(self, values):
            st_v[self.slot, 0] = row_sums(values)

        def send(self, peer):
            n = self.at
            self.copy = send(st_v.at[self.slot, n], st_o.at[self.slot, n], (sec, peer))

        def absorb(self):
            n = self.at
            self.copy.wait_recv()
            st_v[self.slot, n + 1] = st_v[self.slot, n] + st_o[self.slot, n]
            self.at = n + 1

        def value(self):
            return st_v[self.slot, self.at]

    def scale_of(total):
        return lax.rsqrt(total.value() / total_width + EPSILON)

    def forward_chain(h, x, wait_x, v, o, slot, finish_first, finish_second):
        rows = rows_of(h)

        def forward(p, k, emit):
            if k == 0:
                both = contract(v[p, 0, rows, :], local_weights(p), 1, 0)
                for l in range(2):
                    emit(l, both[:, columns(l)])
                return
            for l in range(2):
                lhs = jnp.concatenate(
                    [v[p, k, rows, columns(l)], o[p, k - 1, rows, columns(l)]], axis=1
                )
                emit(l, contract(lhs, stacked(p, k, l), 1, 0))

        def store(p, k):
            def emit(l, value):
                v[p, k, rows, columns(l)] = value.astype(BF16)

            return emit

        total = Total(slot)
        if wait_x is not None:
            wait_x.wait_recv()
        squares = None
        for l in range(2):
            part = x[rows, columns(l)].astype(F32)
            v[0, 0, rows, columns(l)] = (part * gain[:, columns(l)]).astype(BF16)
            squares = part * part if squares is None else squares + part * part
        total.begin(squares)
        for p in range(2):
            forward(p, 0, store(p, 1))
            for k in range(1, factors):
                if p == 1 and k == last and finish_second is None:
                    break
                copy = send(v.at[p, k, rows, :], o.at[p, k - 1, rows, :], (sec, peers[k - 1]))
                if p == 0:
                    total.send(peers[k - 1])
                yield
                copy.wait_recv()
                if p == 0:
                    total.absorb()
                if k < last:
                    forward(p, k, store(p, k + 1))
                elif p == 0:
                    forward(p, k, finish_first(rows, total))
                else:
                    forward(p, k, functools.partial(finish_second, rows))
        yield

    def stash_first(rows, total):
        scale = scale_of(total)
        rs_row[:, rows] = scale
        rs_col[rows, :] = as_column(scale)

        def emit(l, value):
            value = value * rs_col[rows, :]
            pre[rows, columns(l)] = value
            s_v[1, 0, rows, columns(l)] = gelu_value(value).astype(BF16)

        return emit

    def arriving_first(rows, total):
        acc[rows, :] = as_column(scale_of(total))

        def emit(l, value):
            a_v[1, 0, rows, columns(l)] = gelu_value(value * acc[rows, :]).astype(BF16)

        return emit

    def arriving_second(rows, l, value):
        out_act[rows, columns(l)] = (arr[rows, columns(l)].astype(F32) + value).astype(BF16)

    def backward_chain(h, wait_x):
        rows = rows_of(h)
        wait_x.wait_recv()
        total = Total(2 * PARTS + h)
        for p in (1, 0):
            for k in range(last, 0, -1):
                far = p == 1 and k == last
                incoming = b_o.at[p, k - 1, rows, :]
                if far:
                    copy = send(ret.at[rows, :], incoming, (sec, peers[k - 1]))
                else:
                    for l in range(2):
                        both = contract(b_g[p, k, rows, columns(l)], stacked(p, k, l), 1, 1)
                        own[rows, columns(l)] = both[:, columns(0)]
                        b_t[p, k - 1, rows, columns(l)] = both[:, columns(1)].astype(BF16)
                    copy = send(b_t.at[p, k - 1, rows, :], incoming, (sec, peers[k - 1]))
                if p == 0:
                    total.send(peers[k - 1])
                yield
                copy.wait_recv()
                if p == 0:
                    total.absorb()
                if far:
                    if h == 0:
                        far_weights.wait_recv()
                    for l in range(2):
                        lhs = jnp.concatenate(
                            [ret[rows, columns(l)], b_o[p, k - 1, rows, columns(l)]], axis=1
                        )
                        rhs = jnp.concatenate(
                            [selfw[2 * factors - 1, columns(l), :], far_w[columns(l), :]], axis=1
                        )
                        b_g[p, k - 1, rows, columns(l)] = contract(lhs, rhs, 1, 1).astype(BF16)
                else:
                    b_g[p, k - 1, rows, :] = (
                        own[rows, :] + b_o[p, k - 1, rows, :].astype(F32)
                    ).astype(BF16)
            if p == 1:
                dh = contract(b_g[1, 0, rows, :], local_weights(1), 1, 1)
                products = None
                for l in range(2):
                    a = pre[rows, columns(l)]
                    da = dh[:, columns(l)] * gelu_slope(a)
                    products = da * a if products is None else products + da * a
                    b_g[0, last, rows, columns(l)] = (da * rs_col[rows, :]).astype(BF16)
                total.begin(products)
        scale = rs_row[:, rows]
        acc[rows, :] = as_column(scale * scale * total.value() / total_width)
        du = contract(b_g[0, 0, rows, :], local_weights(0), 1, 1)
        for l in range(2):
            part, x = du[:, columns(l)], stash[rows, columns(l)].astype(F32)
            ggain[:, columns(l)] += jnp.sum(part * x, axis=0, keepdims=True)
            value = part * gain[:, columns(l)] - x * acc[rows, :]
            grad_in[rows, columns(l)] = (ret[rows, columns(l)].astype(F32) + value).astype(BF16)
        yield

    def weight_grads(p, k):
        f = p * factors + k
        for l in range(2):
            if p == 1 and k == last:
                rhs = jnp.concatenate([ret[:, columns(l)], b_o[1, last - 1, :, columns(l)]], axis=1)
                both = contract(s_v[1, last, :, columns(l)], rhs, 0, 0).astype(BF16)
                gself[f, columns(l), :] = both[:, columns(0)]
                far_out[columns(l), :] = both[:, columns(1)]
                continue
            if k == 0:
                lhs = s_v[p, 0]
            else:
                lhs = jnp.concatenate([s_v[p, k, :, columns(l)], s_o[p, k - 1, :, columns(l)]], axis=1)
            both = contract(lhs, b_g[p, k, :, columns(l)], 0, 0).astype(BF16)
            mine, theirs = (1, 0) if (k == 0 and l == 1) else (0, 1)
            gself[f, columns(l), :] = both[columns(mine), :]
            gpart[f, columns(l), :] = both[columns(theirs), :]

    far_peer = (sec, peers[last - 1])
    from_ahead, from_behind = [], []
    for h in range(PARTS):
        rows = rows_of(h)
        from_ahead.append(send(gback.at[rows, :], ret.at[rows, :], (behind, tp)))
    for h in range(PARTS):
        rows = rows_of(h)
        from_behind.append(send(sent.at[rows, :], arr.at[rows, :], (ahead, tp)))
    far_weights = send(partw.at[2 * factors - 1], far_w, far_peer)
    ggain[...] = jnp.zeros_like(ggain)
    chains = {}
    for h in range(PARTS):
        chains["S", h] = forward_chain(h, stash, None, s_v, s_o, h, stash_first, None)
        chains["A", h] = forward_chain(
            h, arr, from_behind[h], a_v, a_o, PARTS + h, arriving_first, arriving_second
        )
        chains["B", h] = backward_chain(h, from_ahead[h])
    far_grads = None
    for name, at in order:
        if name == "G":
            weight_grads(*at)
            if at == (1, last):
                far_grads = send(far_out, far_in, far_peer)
        else:
            next(chains[name, at])
    far_grads.wait_recv()
    gpart[2 * factors - 1] = far_in[...]
    for copy in pending:
        copy.wait_send()


def make_order(bits, letters):
    order = []
    done = set()
    count = {name: 0 for name in "SsAaBb"}
    grads = [(1, k) for k in range(bits + 1)] + [(0, k) for k in range(bits, -1, -1)]

    def ready(p, k):
        s, b = min(count["S"], count["s"]), min(count["B"], count["b"])
        if p == 0:
            return s > bits and b >= 2 * bits + 1 - k
        if k == bits:
            return s == 2 * bits and b >= 2
        return s >= bits + 1 + k and b >= bits + 1 - k

    for letter in letters or default_letters(bits):
        if letter == "G":
            todo = [g for g in grads if g not in done and ready(*g)]
            if todo:
                done.add(todo[0])
                order.append(("G", todo[0]))
            continue
        count[letter] += 1
        order.append((letter.upper(), int(letter.islower())))
    for g in grads:
        if g not in done:
            order.append(("G", g))
    return order


def default_letters(bits):
    letters = ""
    for t in range(2 * bits + 1):
        letters += "SBA" if t < 2 * bits else "BA"
        letters += "sba" if t < 2 * bits else "ba"
        if t >= bits:
            letters += "GG"
    return letters


def solution(mesh):
    sections, shards = mesh.shape["section"], mesh.shape["tp"]
    bits = shards.bit_length() - 1

    def per_device(sent_act, stash, grad_back, gain, self_blocks, partner_blocks, block_mask):
        tokens, width = stash.shape[1:]
        factors = self_blocks.shape[2]
        assert width == 2 * BLOCK and factors == bits + 1
        count = 2 * factors
        mask = block_mask[0].reshape(count, 2, 1, 1).astype(BF16)
        partw = (partner_blocks[0].reshape(count, 2, BLOCK, BLOCK) * mask).reshape(count, width, BLOCK)
        copies = PARTS * (2 + 9 * bits) + 2
        vmem = pl.BlockSpec(memory_space=pltpu.VMEM)
        out_act, grad_in, gself, gpart, ggain = pl.pallas_call(
            functools.partial(kernel, sections, bits, make_order(bits, ORDER)),
            out_shape=(
                jax.ShapeDtypeStruct((tokens, width), BF16),
                jax.ShapeDtypeStruct((tokens, width), BF16),
                jax.ShapeDtypeStruct((count, width, BLOCK), BF16),
                jax.ShapeDtypeStruct((count, width, BLOCK), BF16),
                jax.ShapeDtypeStruct((1, width), F32),
            ),
            in_specs=[vmem] * 6,
            out_specs=[vmem] * 5,
            scratch_shapes=[
                pltpu.VMEM((tokens, width), BF16),
                pltpu.VMEM((tokens, width), BF16),
                pltpu.VMEM((2, factors, tokens, width), BF16),
                pltpu.VMEM((2, bits, tokens, width), BF16),
                pltpu.VMEM((2, factors, tokens, width), BF16),
                pltpu.VMEM((2, bits, tokens, width), BF16),
                pltpu.VMEM((2, factors, tokens, width), BF16),
                pltpu.VMEM((2, bits, tokens, width), BF16),
                pltpu.VMEM((2, bits, tokens, width), BF16),
                pltpu.VMEM((tokens, width), F32),
                pltpu.VMEM((tokens, width), F32),
                pltpu.VMEM((tokens, BLOCK), F32),
                pltpu.VMEM((tokens, BLOCK), F32),
                pltpu.VMEM((1, tokens), F32),
                pltpu.VMEM((3 * PARTS, bits + 1, 1, tokens // PARTS), F32),
                pltpu.VMEM((3 * PARTS, bits, 1, tokens // PARTS), F32),
                pltpu.VMEM((width, BLOCK), BF16),
                pltpu.VMEM((width, BLOCK), BF16),
                pltpu.VMEM((width, BLOCK), BF16),
                pltpu.SemaphoreType.DMA((copies,)),
                pltpu.SemaphoreType.DMA((copies,)),
            ],
            compiler_params=pltpu.CompilerParams(
                collective_id=0, has_side_effects=True, vmem_limit_bytes=48 * 2**20
            ),
        )(
            sent_act[0],
            stash[0],
            grad_back[0],
            gain,
            self_blocks[0].reshape(count, width, BLOCK),
            partw,
        )
        gpart = (gpart.reshape(count, 2, BLOCK, BLOCK) * mask).reshape(partner_blocks.shape)
        return out_act[None], grad_in[None], gself.reshape(self_blocks.shape), gpart, ggain

    in_specs = (
        P("section", None, "tp"),
        P("section", None, "tp"),
        P("section", None, "tp"),
        P("section", "tp"),
        P("section", None, None, "tp", None),
        P("section", None, None, "tp", None),
        P("section", None, None, "tp"),
    )
    out_specs = (
        P("section", None, "tp"),
        P("section", None, "tp"),
        P("section", None, None, "tp", None),
        P("section", None, None, "tp", None),
        P("section", "tp"),
    )
    return jax.shard_map(per_device, mesh=mesh, in_specs=in_specs, out_specs=out_specs, check_vma=False)
```

```python
import functools

import jax
import jax.numpy as jnp
from jax import lax
from jax.experimental import pallas as pl
from jax.experimental.pallas import tpu as pltpu
from jax.sharding import PartitionSpec as P

EPSILON = 1e-05
GELU_C = 0.7978845608028654
GELU_A = 0.044715
BLOCK = 128
PARTS = 2
ORDER = "".join(
    [
        "SBsbSBAsbaSBAsbaSBAsbaSB",
        "AsbaSBAsbaGGSBAsbaGGSBAs",
        "baGGSBAsbaGGSBAsbaGGBAba",
        "GGAaGG",
    ]
)
MESH = pl.DeviceIdType.MESH
F32 = jnp.float32
BF16 = jnp.bfloat16


def gelu_value(v):
    inner = GELU_C * (v + GELU_A * v * v * v)
    return 0.5 * v * (1.0 + jnp.tanh(inner))


def gelu_slope(v):
    inner = GELU_C * (v + GELU_A * v * v * v)
    tanh_val = jnp.tanh(inner)
    return 0.5 * (1.0 + tanh_val) + 0.5 * v * (1.0 - tanh_val * tanh_val) * GELU_C * (
        1.0 + 3.0 * GELU_A * v * v
    )


def contract(a, b, da, db):
    return lax.dot_general(a, b, (((da,), (db,)), ((), ())), preferred_element_type=F32)


def columns(l):
    return slice(l * BLOCK, (l + 1) * BLOCK)


def kernel(
    sections,
    bits,
    order,
    sent,
    stash,
    gback,
    gain,
    selfw,
    partw,
    out_act,
    grad_in,
    gself,
    gpart,
    ggain,
    arr,
    ret,
    s_v,
    s_o,
    a_v,
    a_o,
    b_g,
    b_t,
    b_o,
    own,
    pre,
    acc,
    rs_col,
    rs_row,
    st_v,
    st_o,
    far_w,
    far_out,
    far_in,
    near_s,
    near_p,
    near_v,
    send_sem,
    recv_sem,
):
    tokens, width = stash.shape
    part_rows = tokens // PARTS
    factors = bits + 1
    last = factors - 1
    total_width = float((2**bits) * width)
    sec = lax.axis_index("section")
    tp = lax.axis_index("tp")
    ahead = lax.rem(sec + 1, sections)
    behind = lax.rem(sec + sections - 1, sections)
    peers = []
    for j in range(bits):
        m = 2**j
        peers.append(tp + m - 2 * m * ((tp // m) % 2))
    m = 2 ** (bits - 2)
    beside = peers[bits - 1] + m - 2 * m * ((tp // m) % 2)

    barrier = pltpu.get_barrier_semaphore()
    for peer in (*peers, beside):
        pl.semaphore_signal(barrier, inc=1, device_id=(sec, peer), device_id_type=MESH)
    for other in (ahead, behind):
        pl.semaphore_signal(barrier, inc=1, device_id=(other, tp), device_id_type=MESH)
    pl.semaphore_wait(barrier, bits + 3)

    pending = []

    def send(src, dst, where):
        n = len(pending)
        copy = pltpu.make_async_remote_copy(
            src_ref=src,
            dst_ref=dst,
            send_sem=send_sem.at[n],
            recv_sem=recv_sem.at[n],
            device_id=where,
            device_id_type=MESH,
        )
        copy.start()
        pending.append(copy)
        return copy

    def rows_of(h):
        return slice(h * part_rows, (h + 1) * part_rows)

    def local_weights(p):
        f = p * factors
        top = jnp.concatenate([selfw[f, columns(0), :], partw[f, columns(1), :]], axis=1)
        low = jnp.concatenate([partw[f, columns(0), :], selfw[f, columns(1), :]], axis=1)
        return jnp.concatenate([top, low], axis=0)

    def stacked(p, k, l):
        f = p * factors + k
        return jnp.concatenate([selfw[f, columns(l), :], partw[f, columns(l), :]], axis=0)

    def row_sums(values):
        return jnp.sum(values.T, axis=0, keepdims=True)

    def as_column(row):
        return jnp.broadcast_to(row, (BLOCK, part_rows)).T

    class Total:
        def __init__(self, slot):
            self.slot, self.at = slot, 0

        def begin(self, values):
            st_v[self.slot, 0] = row_sums(values)

        def send(self, peer):
            n = self.at
            self.copy = send(st_v.at[self.slot, n], st_o.at[self.slot, n], (sec, peer))

        def absorb(self):
            n = self.at
            self.copy.wait_recv()
            st_v[self.slot, n + 1] = st_v[self.slot, n] + st_o[self.slot, n]
            self.at = n + 1

        def value(self):
            return st_v[self.slot, self.at]

    def scale_of(total):
        return lax.rsqrt(total.value() / total_width + EPSILON)

    def forward_chain(h, x, wait_x, v, o, slot, finish_first, finish_second):
        rows = rows_of(h)

        def forward(p, k, emit):
            if k == 0:
                both = contract(v[p, 0, rows, :], local_weights(p), 1, 0)
                for l in range(2):
                    emit(l, both[:, columns(l)])
                return
            for l in range(2):
                lhs = jnp.concatenate(
                    [v[p, k, rows, columns(l)], o[p, k - 1, rows, columns(l)]], axis=1
                )
                emit(l, contract(lhs, stacked(p, k, l), 1, 0))

        def neighbour(p):
            if p not in near_ready:
                near_ready.append(p)
                for copy in near_weights[p]:
                    copy.wait_recv()
            for l in range(2):
                lhs = jnp.concatenate(
                    [o[p, last - 2, rows, columns(l)], v[p, last - 1, rows, columns(l)]], axis=1
                )
                rhs = jnp.concatenate([near_s[p, columns(l), :], near_p[p, columns(l), :]], axis=0)
                near_v[2 * slot + p, :, columns(l)] = contract(lhs, rhs, 1, 0).astype(BF16)

        def store(p, k):
            def emit(l, value):
                v[p, k, rows, columns(l)] = value.astype(BF16)

            return emit

        total = Total(slot)
        if wait_x is not None:
            wait_x.wait_recv()
        squares = None
        for l in range(2):
            part = x[rows, columns(l)].astype(F32)
            v[0, 0, rows, columns(l)] = (part * gain[:, columns(l)]).astype(BF16)
            squares = part * part if squares is None else squares + part * part
        total.begin(squares)
        for p in range(2):
            if p == 1 and p not in near_weights:
                send_near(p)
            forward(p, 0, store(p, 1))
            for k in range(1, factors):
                if p == 1 and k == last and finish_second is None:
                    break
                if k == last:
                    src, where = near_v.at[2 * slot + p], beside
                else:
                    src, where = v.at[p, k, rows, :], peers[k - 1]
                copy = send(src, o.at[p, k - 1, rows, :], (sec, where))
                if p == 0:
                    total.send(where)
                yield
                copy.wait_recv()
                if p == 0:
                    total.absorb()
                if k == last - 1 and not (p == 1 and finish_second is None):
                    neighbour(p)
                if k < last:
                    forward(p, k, store(p, k + 1))
                elif p == 0:
                    forward(p, k, finish_first(rows, total))
                else:
                    forward(p, k, functools.partial(finish_second, rows))
        yield

    def stash_first(rows, total):
        scale = scale_of(total)
        rs_row[:, rows] = scale
        rs_col[rows, :] = as_column(scale)

        def emit(l, value):
            value = value * rs_col[rows, :]
            pre[rows, columns(l)] = value
            s_v[1, 0, rows, columns(l)] = gelu_value(value).astype(BF16)

        return emit

    def arriving_first(rows, total):
        acc[rows, :] = as_column(scale_of(total))

        def emit(l, value):
            a_v[1, 0, rows, columns(l)] = gelu_value(value * acc[rows, :]).astype(BF16)

        return emit

    def arriving_second(rows, l, value):
        out_act[rows, columns(l)] = (arr[rows, columns(l)].astype(F32) + value).astype(BF16)

    def backward_chain(h, wait_x):
        rows = rows_of(h)
        wait_x.wait_recv()
        total = Total(2 * PARTS + h)
        for p in (1, 0):
            for k in range(last, 0, -1):
                far = p == 1 and k == last
                incoming = b_o.at[p, k - 1, rows, :]
                if far:
                    copy = send(ret.at[rows, :], incoming, (sec, peers[k - 1]))
                else:
                    for l in range(2):
                        both = contract(b_g[p, k, rows, columns(l)], stacked(p, k, l), 1, 1)
                        own[rows, columns(l)] = both[:, columns(0)]
                        b_t[p, k - 1, rows, columns(l)] = both[:, columns(1)].astype(BF16)
                    copy = send(b_t.at[p, k - 1, rows, :], incoming, (sec, peers[k - 1]))
                if p == 0:
                    total.send(peers[k - 1])
                yield
                copy.wait_recv()
                if p == 0:
                    total.absorb()
                if far:
                    if h == 0:
                        far_weights.wait_recv()
                    for l in range(2):
                        lhs = jnp.concatenate(
                            [ret[rows, columns(l)], b_o[p, k - 1, rows, columns(l)]], axis=1
                        )
                        rhs = jnp.concatenate(
                            [selfw[2 * factors - 1, columns(l), :], far_w[columns(l), :]], axis=1
                        )
                        b_g[p, k - 1, rows, columns(l)] = contract(lhs, rhs, 1, 1).astype(BF16)
                else:
                    b_g[p, k - 1, rows, :] = (
                        own[rows, :] + b_o[p, k - 1, rows, :].astype(F32)
                    ).astype(BF16)
            if p == 1:
                dh = contract(b_g[1, 0, rows, :], local_weights(1), 1, 1)
                products = None
                for l in range(2):
                    a = pre[rows, columns(l)]
                    da = dh[:, columns(l)] * gelu_slope(a)
                    products = da * a if products is None else products + da * a
                    b_g[0, last, rows, columns(l)] = (da * rs_col[rows, :]).astype(BF16)
                total.begin(products)
        scale = rs_row[:, rows]
        acc[rows, :] = as_column(scale * scale * total.value() / total_width)
        du = contract(b_g[0, 0, rows, :], local_weights(0), 1, 1)
        for l in range(2):
            part, x = du[:, columns(l)], stash[rows, columns(l)].astype(F32)
            ggain[:, columns(l)] += jnp.sum(part * x, axis=0, keepdims=True)
            value = part * gain[:, columns(l)] - x * acc[rows, :]
            grad_in[rows, columns(l)] = (ret[rows, columns(l)].astype(F32) + value).astype(BF16)
        yield

    def weight_grads(p, k):
        f = p * factors + k
        for l in range(2):
            if p == 1 and k == last:
                rhs = jnp.concatenate([ret[:, columns(l)], b_o[1, last - 1, :, columns(l)]], axis=1)
                both = contract(s_v[1, last, :, columns(l)], rhs, 0, 0).astype(BF16)
                gself[f, columns(l), :] = both[:, columns(0)]
                far_out[columns(l), :] = both[:, columns(1)]
                continue
            if k == 0:
                lhs = s_v[p, 0]
            else:
                lhs = jnp.concatenate([s_v[p, k, :, columns(l)], s_o[p, k - 1, :, columns(l)]], axis=1)
            both = contract(lhs, b_g[p, k, :, columns(l)], 0, 0).astype(BF16)
            mine, theirs = (1, 0) if (k == 0 and l == 1) else (0, 1)
            gself[f, columns(l), :] = both[columns(mine), :]
            gpart[f, columns(l), :] = both[columns(theirs), :]

    far_peer = (sec, peers[last - 1])
    from_ahead, from_behind = [], []
    for h in range(PARTS):
        rows = rows_of(h)
        from_ahead.append(send(gback.at[rows, :], ret.at[rows, :], (behind, tp)))
    for h in range(PARTS):
        rows = rows_of(h)
        from_behind.append(send(sent.at[rows, :], arr.at[rows, :], (ahead, tp)))
    far_weights = send(partw.at[2 * factors - 1], far_w, far_peer)
    near_weights, near_ready = {}, []

    def send_near(p):
        f, where = p * factors + last - 1, (sec, peers[last - 2])
        near_weights[p] = (
            send(selfw.at[f], near_s.at[p], where),
            send(partw.at[f], near_p.at[p], where),
        )

    send_near(0)
    ggain[...] = jnp.zeros_like(ggain)
    chains = {}
    for h in range(PARTS):
        chains["S", h] = forward_chain(h, stash, None, s_v, s_o, h, stash_first, None)
        chains["A", h] = forward_chain(
            h, arr, from_behind[h], a_v, a_o, PARTS + h, arriving_first, arriving_second
        )
        chains["B", h] = backward_chain(h, from_ahead[h])
    far_grads = None
    for name, at in order:
        if name == "G":
            weight_grads(*at)
            if at == (1, last):
                far_grads = send(far_out, far_in, far_peer)
        else:
            next(chains[name, at])
    far_grads.wait_recv()
    gpart[2 * factors - 1] = far_in[...]
    for copy in pending:
        copy.wait_send()


def make_order(bits, letters):
    order = []
    done = set()
    count = {name: 0 for name in "SsAaBb"}
    grads = [(1, k) for k in range(bits + 1)] + [(0, k) for k in range(bits, -1, -1)]

    def ready(p, k):
        s, b = min(count["S"], count["s"]), min(count["B"], count["b"])
        if p == 0:
            return s > bits and b >= 2 * bits + 1 - k
        if k == bits:
            return s == 2 * bits and b >= 2
        return s >= bits + 1 + k and b >= bits + 1 - k

    for letter in letters or default_letters(bits):
        if letter == "G":
            todo = [g for g in grads if g not in done and ready(*g)]
            if todo:
                done.add(todo[0])
                order.append(("G", todo[0]))
            continue
        count[letter] += 1
        order.append((letter.upper(), int(letter.islower())))
    for g in grads:
        if g not in done:
            order.append(("G", g))
    return order


def default_letters(bits):
    letters = ""
    for t in range(2 * bits + 1):
        letters += "SBA" if t < 2 * bits else "BA"
        letters += "sba" if t < 2 * bits else "ba"
        if t >= bits:
            letters += "GG"
    return letters


def solution(mesh):
    sections, shards = mesh.shape["section"], mesh.shape["tp"]
    bits = shards.bit_length() - 1

    def per_device(sent_act, stash, grad_back, gain, self_blocks, partner_blocks, block_mask):
        tokens, width = stash.shape[1:]
        factors = self_blocks.shape[2]
        assert width == 2 * BLOCK and factors == bits + 1
        count = 2 * factors
        mask = block_mask[0].reshape(count, 2, 1, 1).astype(BF16)
        partw = (partner_blocks[0].reshape(count, 2, BLOCK, BLOCK) * mask).reshape(count, width, BLOCK)
        copies = PARTS * (2 + 9 * bits) + 6
        vmem = pl.BlockSpec(memory_space=pltpu.VMEM)
        out_act, grad_in, gself, gpart, ggain = pl.pallas_call(
            functools.partial(kernel, sections, bits, make_order(bits, ORDER)),
            out_shape=(
                jax.ShapeDtypeStruct((tokens, width), BF16),
                jax.ShapeDtypeStruct((tokens, width), BF16),
                jax.ShapeDtypeStruct((count, width, BLOCK), BF16),
                jax.ShapeDtypeStruct((count, width, BLOCK), BF16),
                jax.ShapeDtypeStruct((1, width), F32),
            ),
            in_specs=[vmem] * 6,
            out_specs=[vmem] * 5,
            scratch_shapes=[
                pltpu.VMEM((tokens, width), BF16),
                pltpu.VMEM((tokens, width), BF16),
                pltpu.VMEM((2, factors, tokens, width), BF16),
                pltpu.VMEM((2, bits, tokens, width), BF16),
                pltpu.VMEM((2, factors, tokens, width), BF16),
                pltpu.VMEM((2, bits, tokens, width), BF16),
                pltpu.VMEM((2, factors, tokens, width), BF16),
                pltpu.VMEM((2, bits, tokens, width), BF16),
                pltpu.VMEM((2, bits, tokens, width), BF16),
                pltpu.VMEM((tokens, width), F32),
                pltpu.VMEM((tokens, width), F32),
                pltpu.VMEM((tokens, BLOCK), F32),
                pltpu.VMEM((tokens, BLOCK), F32),
                pltpu.VMEM((1, tokens), F32),
                pltpu.VMEM((3 * PARTS, bits + 1, 1, tokens // PARTS), F32),
                pltpu.VMEM((3 * PARTS, bits, 1, tokens // PARTS), F32),
                pltpu.VMEM((width, BLOCK), BF16),
                pltpu.VMEM((width, BLOCK), BF16),
                pltpu.VMEM((width, BLOCK), BF16),
                pltpu.VMEM((2, width, BLOCK), BF16),
                pltpu.VMEM((2, width, BLOCK), BF16),
                pltpu.VMEM((4 * PARTS, tokens // PARTS, width), BF16),
                pltpu.SemaphoreType.DMA((copies,)),
                pltpu.SemaphoreType.DMA((copies,)),
            ],
            compiler_params=pltpu.CompilerParams(
                collective_id=0, has_side_effects=True, vmem_limit_bytes=48 * 2**20
            ),
        )(
            sent_act[0],
            stash[0],
            grad_back[0],
            gain,
            self_blocks[0].reshape(count, width, BLOCK),
            partw,
        )
        gpart = (gpart.reshape(count, 2, BLOCK, BLOCK) * mask).reshape(partner_blocks.shape)
        return out_act[None], grad_in[None], gself.reshape(self_blocks.shape), gpart, ggain

    in_specs = (
        P("section", None, "tp"),
        P("section", None, "tp"),
        P("section", None, "tp"),
        P("section", "tp"),
        P("section", None, None, "tp", None),
        P("section", None, None, "tp", None),
        P("section", None, None, "tp"),
    )
    out_specs = (
        P("section", None, "tp"),
        P("section", None, "tp"),
        P("section", None, None, "tp", None),
        P("section", None, None, "tp", None),
        P("section", "tp"),
    )
    return jax.shard_map(per_device, mesh=mesh, in_specs=in_specs, out_specs=out_specs, check_vma=False)
```

```python
import functools

import jax
import jax.numpy as jnp
from jax import lax
from jax.experimental import pallas as pl
from jax.experimental.pallas import tpu as pltpu
from jax.sharding import PartitionSpec as P

EPSILON = 1e-05
GELU_C = 0.7978845608028654
GELU_A = 0.044715
BLOCK = 128
PARTS = 2
ORDER = "".join(
    [
        "SBsbSBAsbaSBAsbaSBAsbaSB",
        "AsbaSBAsbaGGSBAsbaGGSBAs",
        "baGGSBAsbaGGSBAsbaGGBAba",
        "GGAaGG",
    ]
)
MESH = pl.DeviceIdType.MESH
F32 = jnp.float32
BF16 = jnp.bfloat16


def gelu_value(v):
    inner = GELU_C * (v + GELU_A * v * v * v)
    return 0.5 * v * (1.0 + jnp.tanh(inner))


def gelu_slope(v):
    inner = GELU_C * (v + GELU_A * v * v * v)
    tanh_val = jnp.tanh(inner)
    return 0.5 * (1.0 + tanh_val) + 0.5 * v * (1.0 - tanh_val * tanh_val) * GELU_C * (
        1.0 + 3.0 * GELU_A * v * v
    )


def contract(a, b, da, db):
    return lax.dot_general(a, b, (((da,), (db,)), ((), ())), preferred_element_type=F32)


def columns(l):
    return slice(l * BLOCK, (l + 1) * BLOCK)


def kernel(
    sections,
    bits,
    order,
    sent,
    stash,
    gback,
    gain,
    selfw,
    raw_partw,
    present,
    out_act,
    grad_in,
    gself,
    gpart,
    ggain,
    arr,
    ret,
    s_v,
    s_o,
    a_v,
    a_o,
    b_g,
    b_t,
    b_o,
    own,
    pre,
    acc,
    rs_col,
    rs_row,
    st_v,
    st_o,
    far_w,
    far_out,
    far_in,
    near_s,
    near_p,
    near_v,
    partw,
    send_sem,
    recv_sem,
):
    tokens, width = stash.shape
    part_rows = tokens // PARTS
    factors = bits + 1
    last = factors - 1
    total_width = float((2**bits) * width)
    sec = lax.axis_index("section")
    tp = lax.axis_index("tp")
    ahead = lax.rem(sec + 1, sections)
    behind = lax.rem(sec + sections - 1, sections)
    peers = []
    for j in range(bits):
        m = 2**j
        peers.append(tp + m - 2 * m * ((tp // m) % 2))
    m = 2 ** (bits - 2)
    beside = peers[bits - 1] + m - 2 * m * ((tp // m) % 2)

    barrier = pltpu.get_barrier_semaphore()
    for peer in (*peers, beside):
        pl.semaphore_signal(barrier, inc=1, device_id=(sec, peer), device_id_type=MESH)
    for other in (ahead, behind):
        pl.semaphore_signal(barrier, inc=1, device_id=(other, tp), device_id_type=MESH)
    pl.semaphore_wait(barrier, bits + 3)

    pending = []

    def send(src, dst, where):
        n = len(pending)
        copy = pltpu.make_async_remote_copy(
            src_ref=src,
            dst_ref=dst,
            send_sem=send_sem.at[n],
            recv_sem=recv_sem.at[n],
            device_id=where,
            device_id_type=MESH,
        )
        copy.start()
        pending.append(copy)
        return copy

    def rows_of(h):
        return slice(h * part_rows, (h + 1) * part_rows)

    def local_weights(p):
        f = p * factors
        top = jnp.concatenate([selfw[f, columns(0), :], partw[f, columns(1), :]], axis=1)
        low = jnp.concatenate([partw[f, columns(0), :], selfw[f, columns(1), :]], axis=1)
        return jnp.concatenate([top, low], axis=0)

    def stacked(p, k, l):
        f = p * factors + k
        return jnp.concatenate([selfw[f, columns(l), :], partw[f, columns(l), :]], axis=0)

    def row_sums(values):
        return jnp.sum(values.T, axis=0, keepdims=True)

    def as_column(row):
        return jnp.broadcast_to(row, (BLOCK, part_rows)).T

    class Total:
        def __init__(self, slot):
            self.slot, self.at = slot, 0

        def begin(self, values):
            st_v[self.slot, 0] = row_sums(values)

        def send(self, peer):
            n = self.at
            self.copy = send(st_v.at[self.slot, n], st_o.at[self.slot, n], (sec, peer))

        def absorb(self):
            n = self.at
            self.copy.wait_recv()
            st_v[self.slot, n + 1] = st_v[self.slot, n] + st_o[self.slot, n]
            self.at = n + 1

        def value(self):
            return st_v[self.slot, self.at]

    def scale_of(total):
        return lax.rsqrt(total.value() / total_width + EPSILON)

    def forward_chain(h, x, wait_x, v, o, slot, finish_first, finish_second):
        rows = rows_of(h)

        def forward(p, k, emit):
            if k == 0:
                both = contract(v[p, 0, rows, :], local_weights(p), 1, 0)
                for l in range(2):
                    emit(l, both[:, columns(l)])
                return
            for l in range(2):
                lhs = jnp.concatenate(
                    [v[p, k, rows, columns(l)], o[p, k - 1, rows, columns(l)]], axis=1
                )
                emit(l, contract(lhs, stacked(p, k, l), 1, 0))

        def neighbour(p):
            if p not in near_ready:
                near_ready.append(p)
                for copy in near_weights[p]:
                    copy.wait_recv()
            for l in range(2):
                lhs = jnp.concatenate(
                    [o[p, last - 2, rows, columns(l)], v[p, last - 1, rows, columns(l)]], axis=1
                )
                rhs = jnp.concatenate([near_s[p, columns(l), :], near_p[p, columns(l), :]], axis=0)
                near_v[2 * slot + p, :, columns(l)] = contract(lhs, rhs, 1, 0).astype(BF16)

        def store(p, k):
            def emit(l, value):
                v[p, k, rows, columns(l)] = value.astype(BF16)

            return emit

        total = Total(slot)
        if wait_x is not None:
            wait_x.wait_recv()
        squares = None
        for l in range(2):
            part = x[rows, columns(l)].astype(F32)
            v[0, 0, rows, columns(l)] = (part * gain[:, columns(l)]).astype(BF16)
            squares = part * part if squares is None else squares + part * part
        total.begin(squares)
        for p in range(2):
            if p == 1 and p not in near_weights:
                send_near(p)
            forward(p, 0, store(p, 1))
            for k in range(1, factors):
                if p == 1 and k == last and finish_second is None:
                    break
                if k == last:
                    src, where = near_v.at[2 * slot + p], beside
                else:
                    src, where = v.at[p, k, rows, :], peers[k - 1]
                copy = send(src, o.at[p, k - 1, rows, :], (sec, where))
                if p == 0:
                    total.send(where)
                yield
                copy.wait_recv()
                if p == 0:
                    total.absorb()
                if k == last - 1 and not (p == 1 and finish_second is None):
                    neighbour(p)
                if k < last:
                    forward(p, k, store(p, k + 1))
                elif p == 0:
                    forward(p, k, finish_first(rows, total))
                else:
                    forward(p, k, functools.partial(finish_second, rows))
        yield

    def stash_first(rows, total):
        scale = scale_of(total)
        rs_row[:, rows] = scale
        rs_col[rows, :] = as_column(scale)

        def emit(l, value):
            value = value * rs_col[rows, :]
            pre[rows, columns(l)] = value
            s_v[1, 0, rows, columns(l)] = gelu_value(value).astype(BF16)

        return emit

    def arriving_first(rows, total):
        acc[rows, :] = as_column(scale_of(total))

        def emit(l, value):
            a_v[1, 0, rows, columns(l)] = gelu_value(value * acc[rows, :]).astype(BF16)

        return emit

    def arriving_second(rows, l, value):
        out_act[rows, columns(l)] = (arr[rows, columns(l)].astype(F32) + value).astype(BF16)

    def backward_chain(h, wait_x):
        rows = rows_of(h)
        wait_x.wait_recv()
        total = Total(2 * PARTS + h)
        for p in (1, 0):
            for k in range(last, 0, -1):
                far = p == 1 and k == last
                incoming = b_o.at[p, k - 1, rows, :]
                if far:
                    copy = send(ret.at[rows, :], incoming, (sec, peers[k - 1]))
                else:
                    for l in range(2):
                        both = contract(b_g[p, k, rows, columns(l)], stacked(p, k, l), 1, 1)
                        own[rows, columns(l)] = both[:, columns(0)]
                        b_t[p, k - 1, rows, columns(l)] = both[:, columns(1)].astype(BF16)
                    copy = send(b_t.at[p, k - 1, rows, :], incoming, (sec, peers[k - 1]))
                if p == 0:
                    total.send(peers[k - 1])
                yield
                copy.wait_recv()
                if p == 0:
                    total.absorb()
                if far:
                    if h == 0:
                        far_weights.wait_recv()
                    for l in range(2):
                        lhs = jnp.concatenate(
                            [ret[rows, columns(l)], b_o[p, k - 1, rows, columns(l)]], axis=1
                        )
                        rhs = jnp.concatenate(
                            [selfw[2 * factors - 1, columns(l), :], far_w[columns(l), :]], axis=1
                        )
                        b_g[p, k - 1, rows, columns(l)] = contract(lhs, rhs, 1, 1).astype(BF16)
                else:
                    b_g[p, k - 1, rows, :] = (
                        own[rows, :] + b_o[p, k - 1, rows, :].astype(F32)
                    ).astype(BF16)
            if p == 1:
                dh = contract(b_g[1, 0, rows, :], local_weights(1), 1, 1)
                products = None
                for l in range(2):
                    a = pre[rows, columns(l)]
                    da = dh[:, columns(l)] * gelu_slope(a)
                    products = da * a if products is None else products + da * a
                    b_g[0, last, rows, columns(l)] = (da * rs_col[rows, :]).astype(BF16)
                total.begin(products)
        scale = rs_row[:, rows]
        acc[rows, :] = as_column(scale * scale * total.value() / total_width)
        du = contract(b_g[0, 0, rows, :], local_weights(0), 1, 1)
        for l in range(2):
            part, x = du[:, columns(l)], stash[rows, columns(l)].astype(F32)
            ggain[:, columns(l)] += jnp.sum(part * x, axis=0, keepdims=True)
            value = part * gain[:, columns(l)] - x * acc[rows, :]
            grad_in[rows, columns(l)] = (ret[rows, columns(l)].astype(F32) + value).astype(BF16)
        yield

    def weight_grads(p, k):
        f = p * factors + k
        for l in range(2):
            if p == 1 and k == last:
                rhs = jnp.concatenate([ret[:, columns(l)], b_o[1, last - 1, :, columns(l)]], axis=1)
                both = contract(s_v[1, last, :, columns(l)], rhs, 0, 0).astype(BF16)
                gself[f, columns(l), :] = both[:, columns(0)]
                far_out[columns(l), :] = both[:, columns(1)]
                continue
            if k == 0:
                lhs = s_v[p, 0]
            else:
                lhs = jnp.concatenate([s_v[p, k, :, columns(l)], s_o[p, k - 1, :, columns(l)]], axis=1)
            both = contract(lhs, b_g[p, k, :, columns(l)], 0, 0).astype(BF16)
            mine, theirs = (1, 0) if (k == 0 and l == 1) else (0, 1)
            gself[f, columns(l), :] = both[columns(mine), :]
            gpart[f, columns(l), :] = both[columns(theirs), :]

    far_peer = (sec, peers[last - 1])
    from_ahead, from_behind = [], []
    for h in range(PARTS):
        rows = rows_of(h)
        from_ahead.append(send(gback.at[rows, :], ret.at[rows, :], (behind, tp)))
    for h in range(PARTS):
        rows = rows_of(h)
        from_behind.append(send(sent.at[rows, :], arr.at[rows, :], (ahead, tp)))
    for f in range(2 * factors):
        for l in range(2):
            blocks = raw_partw[f, columns(l), :].astype(F32)
            partw[f, columns(l), :] = (blocks * present[f, l].astype(F32)).astype(BF16)
    far_weights = send(partw.at[2 * factors - 1], far_w, far_peer)
    near_weights, near_ready = {}, []

    def send_near(p):
        f, where = p * factors + last - 1, (sec, peers[last - 2])
        near_weights[p] = (
            send(selfw.at[f], near_s.at[p], where),
            send(partw.at[f], near_p.at[p], where),
        )

    send_near(0)
    ggain[...] = jnp.zeros_like(ggain)
    chains = {}
    for h in range(PARTS):
        chains["S", h] = forward_chain(h, stash, None, s_v, s_o, h, stash_first, None)
        chains["A", h] = forward_chain(
            h, arr, from_behind[h], a_v, a_o, PARTS + h, arriving_first, arriving_second
        )
        chains["B", h] = backward_chain(h, from_ahead[h])
    far_grads = None
    for name, at in order:
        if name == "G":
            weight_grads(*at)
            if at == (1, last):
                far_grads = send(far_out, far_in, far_peer)
        else:
            next(chains[name, at])
    far_grads.wait_recv()
    gpart[2 * factors - 1] = far_in[...]
    for copy in pending:
        copy.wait_send()


def make_order(bits, letters):
    order = []
    done = set()
    count = {name: 0 for name in "SsAaBb"}
    grads = [(1, k) for k in range(bits + 1)] + [(0, k) for k in range(bits, -1, -1)]

    def ready(p, k):
        s, b = min(count["S"], count["s"]), min(count["B"], count["b"])
        if p == 0:
            return s > bits and b >= 2 * bits + 1 - k
        if k == bits:
            return s == 2 * bits and b >= 2
        return s >= bits + 1 + k and b >= bits + 1 - k

    for letter in letters or default_letters(bits):
        if letter == "G":
            todo = [g for g in grads if g not in done and ready(*g)]
            if todo:
                done.add(todo[0])
                order.append(("G", todo[0]))
            continue
        count[letter] += 1
        order.append((letter.upper(), int(letter.islower())))
    for g in grads:
        if g not in done:
            order.append(("G", g))
    return order


def default_letters(bits):
    letters = ""
    for t in range(2 * bits + 1):
        letters += "SBA" if t < 2 * bits else "BA"
        letters += "sba" if t < 2 * bits else "ba"
        if t >= bits:
            letters += "GG"
    return letters


def solution(mesh):
    sections, shards = mesh.shape["section"], mesh.shape["tp"]
    bits = shards.bit_length() - 1

    def per_device(sent_act, stash, grad_back, gain, self_blocks, partner_blocks, block_mask):
        tokens, width = stash.shape[1:]
        factors = self_blocks.shape[2]
        assert width == 2 * BLOCK and factors == bits + 1
        count = 2 * factors
        mask = block_mask[0].reshape(count, 2, 1, 1).astype(BF16)
        copies = PARTS * (2 + 9 * bits) + 6
        vmem = pl.BlockSpec(memory_space=pltpu.VMEM)
        out_act, grad_in, gself, gpart, ggain = pl.pallas_call(
            functools.partial(kernel, sections, bits, make_order(bits, ORDER)),
            out_shape=(
                jax.ShapeDtypeStruct((tokens, width), BF16),
                jax.ShapeDtypeStruct((tokens, width), BF16),
                jax.ShapeDtypeStruct((count, width, BLOCK), BF16),
                jax.ShapeDtypeStruct((count, width, BLOCK), BF16),
                jax.ShapeDtypeStruct((1, width), F32),
            ),
            in_specs=[vmem] * 6 + [pl.BlockSpec(memory_space=pltpu.SMEM)],
            out_specs=[vmem] * 5,
            scratch_shapes=[
                pltpu.VMEM((tokens, width), BF16),
                pltpu.VMEM((tokens, width), BF16),
                pltpu.VMEM((2, factors, tokens, width), BF16),
                pltpu.VMEM((2, bits, tokens, width), BF16),
                pltpu.VMEM((2, factors, tokens, width), BF16),
                pltpu.VMEM((2, bits, tokens, width), BF16),
                pltpu.VMEM((2, factors, tokens, width), BF16),
                pltpu.VMEM((2, bits, tokens, width), BF16),
                pltpu.VMEM((2, bits, tokens, width), BF16),
                pltpu.VMEM((tokens, width), F32),
                pltpu.VMEM((tokens, width), F32),
                pltpu.VMEM((tokens, BLOCK), F32),
                pltpu.VMEM((tokens, BLOCK), F32),
                pltpu.VMEM((1, tokens), F32),
                pltpu.VMEM((3 * PARTS, bits + 1, 1, tokens // PARTS), F32),
                pltpu.VMEM((3 * PARTS, bits, 1, tokens // PARTS), F32),
                pltpu.VMEM((width, BLOCK), BF16),
                pltpu.VMEM((width, BLOCK), BF16),
                pltpu.VMEM((width, BLOCK), BF16),
                pltpu.VMEM((2, width, BLOCK), BF16),
                pltpu.VMEM((2, width, BLOCK), BF16),
                pltpu.VMEM((4 * PARTS, tokens // PARTS, width), BF16),
                pltpu.VMEM((count, width, BLOCK), BF16),
                pltpu.SemaphoreType.DMA((copies,)),
                pltpu.SemaphoreType.DMA((copies,)),
            ],
            compiler_params=pltpu.CompilerParams(
                collective_id=0, has_side_effects=True, vmem_limit_bytes=48 * 2**20
            ),
        )(
            sent_act[0],
            stash[0],
            grad_back[0],
            gain,
            self_blocks[0].reshape(count, width, BLOCK),
            partner_blocks[0].reshape(count, width, BLOCK),
            block_mask[0].reshape(count, 2),
        )
        gpart = (gpart.reshape(count, 2, BLOCK, BLOCK) * mask).reshape(partner_blocks.shape)
        return out_act[None], grad_in[None], gself.reshape(self_blocks.shape), gpart, ggain

    in_specs = (
        P("section", None, "tp"),
        P("section", None, "tp"),
        P("section", None, "tp"),
        P("section", "tp"),
        P("section", None, None, "tp", None),
        P("section", None, None, "tp", None),
        P("section", None, None, "tp"),
    )
    out_specs = (
        P("section", None, "tp"),
        P("section", None, "tp"),
        P("section", None, None, "tp", None),
        P("section", None, None, "tp", None),
        P("section", "tp"),
    )
    return jax.shard_map(per_device, mesh=mesh, in_specs=in_specs, out_specs=out_specs, check_vma=False)
```
